32 devices in a mesh: grp: 2 (over y), res: 4 (over z), br: 2 (over core), aux: 2 (over x).
Axes of the slice: x: 2, y: 2, z: 4, core: 2. Of those that a mesh axis runs over, the one named last changes fastest.
Arguments:
- homolog_features: bfloat16 [32, 128, 256], P(('grp', 'br', 'aux'), 'res'), parts along dimension 0, may hold values from -6 to 6
- couple_features: bfloat16 [256, 128, 128], P(('grp', 'res'), ('br', 'aux')), parts along dimension 0, may hold values from -6 to 6
- symbol_ids: int32 [32, 128], P(('grp', 'br', 'aux'), 'res'), parts along dimension 0, may hold values from 0 to 22
- entry_present: int32 [32, 128], P(('grp', 'br', 'aux'), 'res'), parts along dimension 0, may hold values 0 or 1
- amino_present: int32 [256], P('grp'), parts along dimension 0, may hold values 0 or 1
- symbol_lookup_matrix: bfloat16 [23, 256], replicated, may hold values from -3 to 3
- horizontal_entry_matrix: bfloat16 [256, 1024], replicated, may hold values from -0.375 to 0.375
- couple_logit_matrix: bfloat16 [128, 8], replicated, may hold values from -40 to 40, as said below
- horizontal_exit_matrix: bfloat16 [256, 256], replicated, may hold values from -0.375 to 0.375
- vertical_entry_matrix: bfloat16 [256, 1024], replicated, may hold values from -0.375 to 0.375
- vertical_exit_matrix: bfloat16 [256, 256], replicated, may hold values from -0.375 to 0.375
- feedforward_first_matrix: bfloat16 [256, 1024], replicated, may hold values from -0.375 to 0.375
- feedforward_second_matrix: bfloat16 [1024, 256], replicated, may hold values from -0.1875 to 0.1875
- trimul_entry_matrix: bfloat16 [128, 640], replicated, may hold values from -0.5 to 0.5
- trimul_exit_matrix: bfloat16 [128, 128], replicated, may hold values from -0.5 to 0.5
Outputs:
- alignment_output: bfloat16 [32, 128, 256], P(('grp', 'br', 'aux'), 'res'), parts along dimension 0
- pair_output: bfloat16 [256, 128, 128], P(('grp', 'res'), ('br', 'aux')), parts along dimension 0
The draws below stay inside these ranges and needn't reach their ends.
There are 2 independent parts, one for each index of `grp`. The reference program is written for one: setup_inputs(seed, part) draws one part's arguments, and reference() takes and returns one part's arrays. A program takes and returns all parts, laid end to end along the dimension named above; an argument that names none is the same for every part. Nothing has to cross between parts.
Inputs may be any that keep to these rules, and one draw needn't show every extreme that they name: `couple_logit_matrix`: a projection of the 128 pair channels onto the 8 heads.
All inputs are finite; a program needn't handle non-finite values. No bound on the sum of `entry_present` on one device may be relied on, other than what follows from the above.
Results may differ from the reference program's by a relative error of at most 0.008.
Values may be sent and summed in bfloat16 or wider, within the bound.
A program may use at most 64 MiB of HBM per device.

```python
import jax
import jax.numpy as jnp
from jax import lax

FEATURE_DEPTH = 256
CZ = 128
FOCI_TOTAL = 8
ATTEND_SPAN = 32
SYMBOL_KINDS = 23
HOMOLOG_TOTAL = 16
AMINO_TOTAL = 128
WIDENED_LAYER = 1024


def draw_couple_logit_matrix(key, part):
    base = jax.random.normal(jax.random.fold_in(key, 11), (CZ, FOCI_TOTAL), jnp.float32) * CZ ** (-0.5)
    return base.astype(jnp.bfloat16)


def plant(values, key, low, top_value):
    shape = values.shape
    spot = [jax.random.randint(jax.random.fold_in(key, axis), (), 0, shape[axis]) for axis in range(len(shape))]
    values = values.at[tuple(spot)].set(low)
    longest = shape.index(max(shape))
    spot[longest] = (spot[longest] + 1) % shape[longest]
    return values.at[tuple(spot)].set(top_value)


def level_of(own_key, dims, split, least, largest):
    def one(dim, parts):
        draws = jax.random.uniform(jax.random.fold_in(jax.random.fold_in(own_key, 6), dim), (parts,), jnp.float32, least / len(split), largest / len(split))
        return jnp.repeat(jnp.exp(draws), dims[dim] // parts).reshape((-1,) + (1,) * (len(dims) - dim - 1))

    level = one(*split[0])
    for cut in split[1:]:
        level = level * one(*cut)
    return level


def gaussian(key, extent, spread, reach, pieces=(), kind=jnp.bfloat16):
    array = jax.random.normal(key, extent, jnp.float32) * spread
    if len(pieces) > 0:
        array = level_of(key, extent, pieces, -0.22, 0.18) * array
    return jnp.clip(array, min=-reach, max=reach).astype(kind)


def setup_inputs(seed: int = 0, part: int = 0) -> dict:
    key_list = jax.random.split(jax.random.key(seed), 16)
    own_keys = jax.random.split(jax.random.fold_in(key_list[15], part), 16)
    homolog_features = gaussian(own_keys[0], (HOMOLOG_TOTAL, AMINO_TOTAL, FEATURE_DEPTH), 1.0, 6.0, ((0, 4), (1, 4)))
    couple_features = gaussian(own_keys[1], (AMINO_TOTAL, AMINO_TOTAL, CZ), 1.0, 6.0, ((0, 4), (1, 4)))
    symbol_ids = plant(jax.random.randint(own_keys[2], (HOMOLOG_TOTAL, AMINO_TOTAL), 0, SYMBOL_KINDS), jax.random.fold_in(own_keys[2], 1), 0, SYMBOL_KINDS - 1).astype(jnp.int32)
    entry_present = plant((jax.random.randint(own_keys[3], (HOMOLOG_TOTAL, AMINO_TOTAL), 0, 4) < 3).astype(jnp.int32), jax.random.fold_in(own_keys[3], 1), 0, 1)
    amino_present = plant((jax.random.randint(own_keys[4], (AMINO_TOTAL,), 0, 8) < 7).astype(jnp.int32), jax.random.fold_in(own_keys[4], 1), 0, 1)
    symbol_lookup_matrix = gaussian(key_list[5], (SYMBOL_KINDS, FEATURE_DEPTH), 0.5, 3.0)
    horizontal_entry_matrix = gaussian(key_list[6], (FEATURE_DEPTH, 4 * FEATURE_DEPTH), FEATURE_DEPTH ** -0.5, 0.375)
    couple_logit_matrix = draw_couple_logit_matrix(jax.random.fold_in(key_list[15], 71), part)
    horizontal_exit_matrix = gaussian(key_list[8], (FEATURE_DEPTH, FEATURE_DEPTH), FEATURE_DEPTH ** -0.5, 0.375)
    vertical_entry_matrix = gaussian(key_list[9], (FEATURE_DEPTH, 4 * FEATURE_DEPTH), FEATURE_DEPTH ** -0.5, 0.375)
    vertical_exit_matrix = gaussian(key_list[10], (FEATURE_DEPTH, FEATURE_DEPTH), FEATURE_DEPTH ** -0.5, 0.375)
    feedforward_first_matrix = gaussian(key_list[11], (FEATURE_DEPTH, WIDENED_LAYER), FEATURE_DEPTH ** -0.5, 0.375)
    feedforward_second_matrix = gaussian(key_list[12], (WIDENED_LAYER, FEATURE_DEPTH), WIDENED_LAYER ** -0.5, 0.1875)
    trimul_entry_matrix = gaussian(key_list[13], (CZ, 5 * CZ), CZ ** -0.5, 0.5)
    trimul_exit_matrix = gaussian(key_list[14], (CZ, CZ), CZ ** -0.5, 0.5)
    return dict(homolog_features=homolog_features, couple_features=couple_features, symbol_ids=symbol_ids, entry_present=entry_present, amino_present=amino_present, symbol_lookup_matrix=symbol_lookup_matrix, horizontal_entry_matrix=horizontal_entry_matrix, couple_logit_matrix=couple_logit_matrix, horizontal_exit_matrix=horizontal_exit_matrix, vertical_entry_matrix=vertical_entry_matrix, vertical_exit_matrix=vertical_exit_matrix, feedforward_first_matrix=feedforward_first_matrix, feedforward_second_matrix=feedforward_second_matrix, trimul_entry_matrix=trimul_entry_matrix, trimul_exit_matrix=trimul_exit_matrix)


epsilon = 1e-05
masked_fill_value = 1000000000.0

def normalize(inputs):
    values = inputs.astype(jnp.float32)
    average = lax.optimization_barrier(jnp.mean(values, axis=-1, keepdims=True))
    centred = values - average
    variance = lax.optimization_barrier(jnp.mean(centred * centred, axis=-1, keepdims=True))
    return centred * lax.rsqrt(variance + epsilon)

def apply_projection(row_block, weight):
    flattened = row_block.reshape(-1, row_block.shape[-1])
    result = jnp.dot(flattened, weight, preferred_element_type=jnp.float32)
    return result.reshape(row_block.shape[:-1] + (weight.shape[1],))

def attend(queries, key_rows, value_rows, bias_block, penalty):
    scores = jnp.einsum('qhd,khd->hqk', queries.astype(jnp.float32), key_rows.astype(jnp.float32)) * ATTEND_SPAN ** (-0.5)
    scores = scores + bias_block + penalty
    row_max = lax.optimization_barrier(jnp.max(scores, axis=-1, keepdims=True))
    powers = jnp.exp(scores - row_max)
    weights = (powers / lax.optimization_barrier(jnp.sum(powers, axis=-1, keepdims=True))).astype(jnp.bfloat16)
    return jnp.einsum('hqk,khd->qhd', weights.astype(jnp.float32), value_rows.astype(jnp.float32))

def reference(homolog_features, couple_features, symbol_ids, entry_present, amino_present, symbol_lookup_matrix, horizontal_entry_matrix, couple_logit_matrix, horizontal_exit_matrix, vertical_entry_matrix, vertical_exit_matrix, feedforward_first_matrix, feedforward_second_matrix, trimul_entry_matrix, trimul_exit_matrix):
    indicator_symbols = (symbol_ids[..., None] == jnp.arange(SYMBOL_KINDS, dtype=jnp.int32)[None, None, :]).astype(jnp.float32)
    symbol_vectors = homolog_features.astype(jnp.float32) + jnp.einsum('zas,sv->zav', indicator_symbols, symbol_lookup_matrix.astype(jnp.float32))
    normed_first = normalize(symbol_vectors).astype(jnp.bfloat16)
    horizontal_combined = apply_projection(normed_first, horizontal_entry_matrix)
    horizontal_queries = horizontal_combined[..., :FEATURE_DEPTH].astype(jnp.bfloat16).reshape(HOMOLOG_TOTAL, AMINO_TOTAL, FOCI_TOTAL, ATTEND_SPAN)
    horizontal_keyset = horizontal_combined[..., FEATURE_DEPTH:2 * FEATURE_DEPTH].astype(jnp.bfloat16).reshape(HOMOLOG_TOTAL, AMINO_TOTAL, FOCI_TOTAL, ATTEND_SPAN)
    horizontal_payload = horizontal_combined[..., 2 * FEATURE_DEPTH:3 * FEATURE_DEPTH].astype(jnp.bfloat16).reshape(HOMOLOG_TOTAL, AMINO_TOTAL, FOCI_TOTAL, ATTEND_SPAN)
    horizontal_sigmoid = jax.nn.sigmoid(horizontal_combined[..., 3 * FEATURE_DEPTH:])
    pair_norm = normalize(couple_features).astype(jnp.bfloat16)
    pair_bias = apply_projection(pair_norm, couple_logit_matrix).transpose(2, 0, 1)
    key_mask_penalty = masked_fill_value * (entry_present.astype(jnp.float32) - 1.0)

    def one_row(items):
        queries, key_rows, value_rows, penalty = items
        return attend(queries, key_rows, value_rows, pair_bias, penalty[None, None, :])
    horizontal_context = lax.map(one_row, (horizontal_queries, horizontal_keyset, horizontal_payload, key_mask_penalty))
    horizontal_result = (horizontal_sigmoid * horizontal_context.reshape(HOMOLOG_TOTAL, AMINO_TOTAL, FEATURE_DEPTH)).astype(jnp.bfloat16)
    after_row = symbol_vectors + apply_projection(horizontal_result, horizontal_exit_matrix)
    normed_second = normalize(after_row).astype(jnp.bfloat16)
    vertical_combined = apply_projection(normed_second, vertical_entry_matrix)
    vertical_queries = vertical_combined[..., :FEATURE_DEPTH].astype(jnp.bfloat16).reshape(HOMOLOG_TOTAL, AMINO_TOTAL, FOCI_TOTAL, ATTEND_SPAN)
    vertical_keyset = vertical_combined[..., FEATURE_DEPTH:2 * FEATURE_DEPTH].astype(jnp.bfloat16).reshape(HOMOLOG_TOTAL, AMINO_TOTAL, FOCI_TOTAL, ATTEND_SPAN)
    vertical_payload = vertical_combined[..., 2 * FEATURE_DEPTH:3 * FEATURE_DEPTH].astype(jnp.bfloat16).reshape(HOMOLOG_TOTAL, AMINO_TOTAL, FOCI_TOTAL, ATTEND_SPAN)
    vertical_sigmoid = jax.nn.sigmoid(vertical_combined[..., 3 * FEATURE_DEPTH:])

    def one_column(items):
        queries, key_rows, value_rows, penalty = items
        return attend(queries, key_rows, value_rows, jnp.zeros((1, 1, 1), jnp.float32), penalty[None, None, :])
    vertical_context = lax.map(one_column, (vertical_queries.transpose(1, 0, 2, 3), vertical_keyset.transpose(1, 0, 2, 3), vertical_payload.transpose(1, 0, 2, 3), key_mask_penalty.T))
    vertical_result = (vertical_sigmoid * vertical_context.transpose(1, 0, 2, 3).reshape(HOMOLOG_TOTAL, AMINO_TOTAL, FEATURE_DEPTH)).astype(jnp.bfloat16)
    after_column_update = after_row + apply_projection(vertical_result, vertical_exit_matrix)
    normed_third = normalize(after_column_update).astype(jnp.bfloat16)
    hidden_units = jax.nn.relu(apply_projection(normed_third, feedforward_first_matrix)).astype(jnp.bfloat16)
    alignment_output = (after_column_update + apply_projection(hidden_units, feedforward_second_matrix)).astype(jnp.bfloat16)
    tri_all = apply_projection(pair_norm, trimul_entry_matrix)
    valid_res = amino_present.astype(jnp.float32)
    pair_valid = (valid_res[:, None] * valid_res[None, :])[..., None]
    left_side = (jax.nn.sigmoid(tri_all[..., CZ:2 * CZ]) * tri_all[..., :CZ] * pair_valid).astype(jnp.bfloat16)
    right_side = (jax.nn.sigmoid(tri_all[..., 3 * CZ:4 * CZ]) * tri_all[..., 2 * CZ:3 * CZ] * pair_valid).astype(jnp.bfloat16)
    out_gate = jax.nn.sigmoid(tri_all[..., 4 * CZ:])
    product = jnp.einsum('kic,kjc->ijc', left_side.astype(jnp.float32), right_side.astype(jnp.float32)).astype(jnp.bfloat16)
    normed_final = normalize(product).astype(jnp.bfloat16)
    pair_output = (couple_features.astype(jnp.float32) + out_gate * apply_projection(normed_final, trimul_exit_matrix)).astype(jnp.bfloat16)
    return (alignment_output, pair_output)
```

```python
import functools
import types

import jax
import jax.numpy as jnp
from jax import lax
from jax.experimental import pallas as pl
from jax.experimental.pallas import tpu as pltpu
from jax.sharding import PartitionSpec as P

epsilon = 1e-05
masked_fill_value = 1000000000.0
MESH = pl.DeviceIdType.MESH
f32 = jnp.float32
bf16 = jnp.bfloat16


def normalize(inputs, axis=-1):
    values = inputs.astype(f32)
    average = jnp.mean(values, axis=axis, keepdims=True)
    centred = values - average
    variance = jnp.mean(centred * centred, axis=axis, keepdims=True)
    return centred * lax.rsqrt(variance + epsilon)


def dot(a, b, contract):
    return lax.dot_general(a, b, (contract, ((), ())), preferred_element_type=f32)


class Peers:
    def __init__(self, sizes):
        self.R, self.BR, self.AX = sizes
        self.r = lax.axis_index("res")
        self.b = lax.axis_index("br")
        self.x = lax.axis_index("aux")

    def res(self, d):
        return lax.rem(self.r + d, self.R)

    def br(self, d):
        return lax.rem(self.b + d, self.BR)

    def aux(self, d):
        return lax.rem(self.x + d, self.AX)

    def res_back(self, d):
        return lax.rem(self.r + self.R - d, self.R)

    def aux_back(self, d):
        return lax.rem(self.x + self.AX - d, self.AX)

    def group(self):
        return [(bo, a) for bo in range(self.BR) for a in range(self.AX) if (bo, a) != (0, 0)]

    def greet(self):
        semaphore = pltpu.get_barrier_semaphore()
        for d in range(1, self.R):
            pl.semaphore_signal(semaphore, inc=1, device_id={"res": self.res(d)}, device_id_type=MESH)
        for bo, a in self.group():
            pl.semaphore_signal(
                semaphore, inc=1, device_id={"br": self.br(bo), "aux": self.aux(a)}, device_id_type=MESH
            )

    def met(self):
        pl.semaphore_wait(pltpu.get_barrier_semaphore(), self.R - 1 + self.BR * self.AX - 1)


def remote(src, dst, send, recv, device):
    copy = pltpu.make_async_remote_copy(
        src_ref=src, dst_ref=dst, send_sem=send, recv_sem=recv, device_id=device, device_id_type=MESH
    )
    copy.start()
    return copy


def iota(shape, axis):
    return lax.broadcasted_iota(jnp.int32, shape, axis)


def by_head(rows, heads):
    n, width = rows.shape
    mask = (iota((heads, width), 1) // (width // heads) == iota((heads, width), 0)).astype(f32)
    return (rows[:, None, :] * mask[None]).reshape(n * heads, width)


def from_head(rows, heads):
    n, width = rows.shape
    mask = (iota((heads, width), 1) // (width // heads) == iota((heads, width), 0)).astype(f32)
    return jnp.sum(rows.reshape(n // heads, heads, width) * mask[None], axis=1)


def attend(scores, values, heads):
    powers = jnp.exp(scores - jnp.max(scores, axis=-1, keepdims=True))
    total = jnp.sum(powers, axis=-1, keepdims=True)
    mixed = dot(powers.astype(bf16), values, ((1,), (0,)))
    return from_head(mixed / total, heads)


def joined(pieces, lanes):
    per_tile = 128 // lanes
    tiles = []
    for first in range(0, len(pieces), per_tile):
        tile = pieces[first]
        group = iota(tile.shape, 1) // lanes
        for k in range(1, min(per_tile, len(pieces) - first)):
            tile = jnp.where(group == k, pieces[first + k], tile)
        tiles.append(tile)
    return tiles[0] if len(tiles) == 1 else jnp.concatenate(tiles, axis=1)


def block_kernel(
    sizes, dims,
    homolog, couple, symbols, entries, amino, table, logit, tri_in, tri_exit,
    row_in_far, row_exit_far, col_in_far, col_exit_far, feed_first_far, feed_second_far,
    alignment, pair,
    rows_own, bias_own, left_own, right_own, keys_own, product_own,
    rows_all, row_present, bias_all, col_present, left_all, right_all, keys_all, product_all,
    row_in, row_exit, col_in, col_exit, feed_first, feed_second, present,
    embedded_s, pair_norm_s, gate_s, bias_s, key_value_s, left_s, right_s, product_s, update_s, context_s,
    res_send, res_recv, grp_send, grp_recv, aux_send, aux_recv, br_send, br_recv,
    across_send, across_recv, over_send, over_recv, weight_sem,
):
    p = Peers(sizes)
    R, BR, AX = sizes
    B = BR * AX
    S, A, F, H, I, J, C, per, T, N = dims
    scale = (F // H) ** (-0.5)
    Q = 128 // J
    M = J // Q
    p.greet()
    weights = []
    for n, (far, near) in enumerate(
        (
            (row_in_far, row_in),
            (row_exit_far, row_exit),
            (col_in_far, col_in),
            (col_exit_far, col_exit),
            (feed_first_far, feed_first),
            (feed_second_far, feed_second),
        )
    ):
        weights.append(pltpu.make_async_copy(far, near, weight_sem.at[n]))
        weights[n].start()
    sent = []
    arriving = {"rows": [], "bias": [], "right": [], "left": [], "keys": [], "product": []}

    pair_norm = normalize(couple[...]).astype(bf16)
    pair_norm_s[...] = pair_norm
    alive = jnp.broadcast_to(amino[...].astype(f32), (8, amino.shape[1])).astype(bf16)
    residue = iota((amino.shape[1], I * J), 0)
    flat = iota((amino.shape[1], I * J), 1)
    row_pick = (residue == p.r * I + flat // J).astype(f32).astype(bf16)
    col_pick = (residue == (p.b * AX + p.x) * J + flat % J).astype(f32).astype(bf16)
    pair_valid = (dot(alive, row_pick, ((1,), (0,))) * dot(alive, col_pick, ((1,), (0,))))[:1]
    turned_in = [jnp.transpose(tri_in[:, n * C : (n + 1) * C].astype(f32)).astype(bf16) for n in range(4)]
    for side, own in ((0, left_own), (1, right_own)):
        value = dot(turned_in[2 * side], pair_norm, ((1,), (1,)))
        sigma = jax.nn.sigmoid(dot(turned_in[2 * side + 1], pair_norm, ((1,), (1,))))
        value = sigma * value * pair_valid
        for n in range(R):
            for t in range(T):
                own[n, t] = value[n * per : (n + 1) * per, t * 128 : (t + 1) * 128].astype(bf16)
    bias_own[...] = dot(jnp.transpose(logit[...].astype(f32)).astype(bf16), pair_norm, ((1,), (1,)))
    here = entries[...].astype(f32)
    present[...] = jnp.zeros_like(present)
    present[0, :S, :] = jnp.concatenate([here] * (128 // A), axis=1)
    for g in range(A // N):
        pieces = [here[s : s + 1, g * N : (g + 1) * N] for s in range(S)]
        present[1, g : g + 1, :] = jnp.concatenate(pieces * (128 // (S * N)), axis=1)
    tokens = table.shape[0]
    for s in range(S):
        chosen = (iota((tokens, A), 0) == symbols[s : s + 1, :]).astype(f32)
        context_s[s * A : (s + 1) * A, :] = dot(jnp.transpose(chosen).astype(bf16), table[...], ((1,), (0,)))
    embedded = homolog[...].astype(f32) + context_s[...]
    embedded_s[...] = embedded
    normed_first = normalize(embedded).astype(bf16)
    rows_own[...] = normed_first

    p.met()

    def relay(d, a):
        origin = (p.b, p.aux_back(a), p.res_back(d))
        src = left_own.at[p.r] if (d, a) == (0, 0) else left_all.at[origin]
        for bo in range(1, BR):
            copy = remote(
                src, left_all.at[origin], br_send.at[d, a, bo], br_recv.at[d, a, bo], {"br": p.br(bo)}
            )
            sent.append(copy)
            arriving["left"].append(copy)

    def spread(d):
        origin = (p.b, p.x, p.res_back(d))
        src = left_own.at[p.r] if d == 0 else left_all.at[origin]
        copies = {}
        for a in range(1, AX):
            copies[a] = remote(
                src, left_all.at[origin], aux_send.at[d, a], aux_recv.at[d, a], {"aux": p.aux(a)}
            )
            sent.append(copies[a])
        relay(d, 0)
        return copies

    def to_res(index, kind, pairs):
        for d in range(1, R):
            for n, (src, dst) in enumerate(pairs(p.res(d))):
                copy = remote(
                    src, dst, res_send.at[index + n, d], res_recv.at[index + n, d], {"res": p.res(d)}
                )
                sent.append(copy)
                arriving[kind].append(copy)

    lefts = {}
    for d in range(1, R):
        lefts[d] = remote(
            left_own.at[p.res(d)], left_all.at[p.b, p.x, p.r], res_send.at[0, d], res_recv.at[0, d],
            {"res": p.res(d)},
        )
        sent.append(lefts[d])
    spreads = {0: spread(0)}
    to_res(1, "rows", lambda to: ((rows_own, rows_all.at[p.r]), (present.at[0], row_present.at[p.r])))
    for n, (bo, a) in enumerate(p.group()):
        to = {"br": p.br(bo), "aux": p.aux(a)}
        for m, (src, dst) in enumerate(((bias_own, bias_all), (present.at[1], col_present))):
            copy = remote(src, dst.at[p.b, p.x], grp_send.at[m, n], grp_recv.at[m, n], to)
            sent.append(copy)
            arriving["bias"].append(copy)
    to_res(3, "right", lambda to: ((right_own.at[to], right_all.at[p.r]),))
    rows_all[p.r] = rows_own[...]
    row_present[p.r] = present[0]
    bias_all[p.b, p.x] = bias_own[...]
    col_present[p.b, p.x] = present[1]
    left_all[p.b, p.x, p.r] = left_own[p.r]
    right_all[p.r] = right_own[p.r]

    weights[0].wait()
    query = dot(normed_first, row_in[:, :F], ((1,), (0,))).astype(bf16).astype(f32)
    row_gate = jax.nn.sigmoid(dot(normed_first, row_in[:, 3 * F :], ((1,), (0,))))
    gate_s[...] = jax.nn.sigmoid(dot(pair_norm, tri_in[:, 4 * C :], ((1,), (0,))))

    for d in range(1, R):
        lefts[d].wait_recv()
        spreads[d] = spread(d)
    for copy in arriving["bias"]:
        copy.wait_recv()
    for t in range(T):
        for q in range(Q):
            pieces = []
            for b in range(B):
                tile = bias_all[b // AX, b % AX, :, t * 128 : (t + 1) * 128]
                turn = (b - q) % Q * J
                pieces.append(pltpu.roll(tile, turn, 1) if turn else tile)
            row = (t * Q + q) * H
            bias_s[row : row + H, :] = joined(pieces, J)
    for d in range(R):
        for a in range(1, AX):
            spreads[d][a].wait_recv()
            relay(d, a)

    for copy in arriving["rows"]:
        copy.wait_recv()
    key_value_s[...] = (
        dot(rows_all[...].reshape(R * S * A, F), row_in[:, F : 3 * F], ((1,), (0,)))
        .astype(bf16)
        .reshape(R, S * A, 2 * F)
    )
    presence = joined([row_present[n] for n in range(R)], A)
    for s in range(S):
        mine = slice(s * A, (s + 1) * A)
        keys = key_value_s[:, mine, :F].reshape(R * A, F)
        values = key_value_s[:, mine, F:].reshape(R * A, F)
        scores = dot(by_head(query[mine], H).astype(bf16), keys, ((1,), (1,))) * scale
        scores = scores + bias_s[...] + masked_fill_value * (presence[s : s + 1] - 1.0)
        context_s[mine, :] = attend(scores, values, H)
    weights[1].wait()
    weights[2].wait()
    row_mix = (row_gate * context_s[...]).astype(bf16)
    after_row = embedded_s[...] + dot(row_mix, row_exit[...], ((1,), (0,)))
    normed_second = normalize(after_row).astype(bf16)
    keys_own[...] = dot(normed_second, col_in[:, F : 3 * F], ((1,), (0,))).astype(bf16).reshape(S, A, 2 * F)
    query = dot(normed_second, col_in[:, :F], ((1,), (0,))).astype(bf16).astype(f32)
    col_gate = jax.nn.sigmoid(dot(normed_second, col_in[:, 3 * F :], ((1,), (0,))))

    def pass_on(a):
        origin = (p.b, p.aux_back(a))
        src = keys_own if a == 0 else keys_all.at[origin]
        for bo in range(1, BR):
            copy = remote(src, keys_all.at[origin], over_send.at[a, bo], over_recv.at[a, bo], {"br": p.br(bo)})
            sent.append(copy)
            arriving["keys"].append(copy)

    across = {}
    for a in range(1, AX):
        across[a] = remote(
            keys_own, keys_all.at[p.b, p.x], across_send.at[a], across_recv.at[a], {"aux": p.aux(a)}
        )
        sent.append(across[a])
    pass_on(0)
    keys_all[p.b, p.x] = keys_own[...]

    for copy in arriving["right"]:
        copy.wait_recv()
    right_s[...] = right_all[...].astype(f32).reshape(R * T * per, 128)
    for copy in arriving["left"]:
        copy.wait_recv()
    for b in range(B):
        left_s[b] = left_all[b // AX, b % AX].astype(f32).reshape(R * T * per, 128)
    wide = iota((J, 128), 1) // J
    lane = iota((M, 128), 1)

    def channel(c, carry):
        pick = pl.ds(c, R * T, stride=per)
        right = jnp.transpose(right_s[pick, :]).astype(bf16)
        lefts = jnp.concatenate([left_s[b, pick, :].astype(bf16) for b in range(B)], axis=1)
        grid = dot(right, lefts, ((1,), (0,)))
        for b in range(B):
            tile = grid[:, b * 128 : (b + 1) * 128]
            folded = tile[:J]
            for q in range(1, Q):
                folded = jnp.where(wide == q, tile[q * J : (q + 1) * J], folded)
            pieces = [folded[g * M : (g + 1) * M] for g in range(Q)]
            turn = J
            while turn < 128:
                low = (lane & turn) == 0
                pieces = [
                    jnp.where(low, pieces[k], pieces[k + 1])
                    + pltpu.roll(jnp.where(low, pieces[k + 1], pieces[k]), turn, 1)
                    for k in range(0, len(pieces), 2)
                ]
                turn *= 2
            product_s[b, pl.ds(pl.multiple_of(c * M, M), M), :] = pieces[0]
        return carry

    lax.fori_loop(0, per, channel, 0, unroll=4)
    product_own[...] = product_s[...].astype(bf16)
    for a in range(1, AX):
        across[a].wait_recv()
        pass_on(a)
    to_res(4, "product", lambda to: ((product_own.at[to], product_all.at[p.r]),))
    product_all[p.r] = product_own[p.r]

    for copy in arriving["keys"]:
        copy.wait_recv()
    presence = joined([col_present[b // AX, b % AX] for b in range(B)], S * N)
    for g in range(A // N):
        keys = keys_all[:, :, :, g * N : (g + 1) * N, :F].reshape(B * S * N, F)
        values = keys_all[:, :, :, g * N : (g + 1) * N, F:].reshape(B * S * N, F)
        rows = jnp.concatenate([query[s * A + g * N : s * A + (g + 1) * N] for s in range(S)], axis=0)
        scores = dot(by_head(rows, H).astype(bf16), keys, ((1,), (1,))) * scale
        scores = scores + masked_fill_value * (presence[g : g + 1] - 1.0)
        scores = jnp.where(iota(scores.shape, 0) // H % N == iota(scores.shape, 1) % N, scores, -1e30)
        context = attend(scores, values, H)
        for s in range(S):
            context_s[s * A + g * N : s * A + (g + 1) * N, :] = context[s * N : (s + 1) * N]
    for n in (3, 4, 5):
        weights[n].wait()
    col_mix = (col_gate * context_s[...]).astype(bf16)
    after_col = after_row + dot(col_mix, col_exit[...], ((1,), (0,)))
    normed_third = normalize(after_col).astype(bf16)
    hidden = jnp.maximum(dot(normed_third, feed_first[...], ((1,), (0,))), 0.0).astype(bf16)
    alignment[...] = (after_col + dot(hidden, feed_second[...], ((1,), (0,)))).astype(bf16)

    for copy in arriving["product"]:
        copy.wait_recv()
    normed = normalize(product_all[...].astype(f32).reshape(C, M, 128), axis=0)
    final_s = left_s.at[0]
    final_s[: C * M, :] = normed.reshape(C * M, 128)
    for m in range(M):
        turned = jnp.transpose(final_s[pl.ds(m, C, stride=M), :]).astype(bf16)
        update = dot(turned, tri_exit[...], ((1,), (0,)))
        for g in range(Q):
            update_s[pl.ds(g * M + m, I, stride=J), :] = update[g * I : (g + 1) * I]
    pair[...] = (couple[...].astype(f32) + gate_s[...] * update_s[...]).astype(bf16)
    for copy in sent:
        copy.wait_send()


def lane_exchange(pieces, width):
    count = len(pieces)
    step = 1
    while step < count:
        lower = (iota(pieces[0].shape, pieces[0].ndim - 1) // width // step) % 2 == 0
        axis = pieces[0].ndim - 1
        turned = list(pieces)
        for n in range(count):
            if n // step % 2 == 0:
                first, second = pieces[n], pieces[n + step]
                turned[n] = jnp.where(lower, first, pltpu.roll(second, step * width, axis))
                turned[n + step] = jnp.where(lower, pltpu.roll(first, 128 - step * width, axis), second)
        pieces = turned
        step *= 2
    return pieces


def exchange_kernel(sizes, dims, names, *refs):
    v = types.SimpleNamespace(**dict(zip(names, refs, strict=True)))
    p = Peers(sizes)
    R, BR, AX = sizes
    B = BR * AX
    D = R * B
    S, A, F, H, I, J, C, P4, T, N, rounds = dims
    scale = (F // H) ** (-0.5)
    Q = 128 // J
    M = J // Q
    peers = [(d, bo, a) for d in far_first(R) for bo in range(BR) for a in range(AX) if (d, bo, a) != (0, 0, 0)]
    loads = {}
    for n, name in enumerate(INPUTS):
        loads[name] = pltpu.make_async_copy(getattr(v, name + "_far"), getattr(v, name), v.load_sem.at[n])
        loads[name].start()
    barrier = pltpu.get_barrier_semaphore()
    for d, bo, a in peers:
        pl.semaphore_signal(
            barrier, inc=1, device_id={"res": p.res(d), "br": p.br(bo), "aux": p.aux(a)}, device_id_type=MESH
        )
    sent = []
    arriving = {"rows": [], "bias": [], "keys": []}

    def chosen_weights(h, gate):
        row = iota((2 * P4 * D, 1), 0)
        want = (2 * (row // P4 % 2) + gate) * C + h * P4 * D + row // (2 * P4) * P4 + row % P4
        pick = (iota((2 * P4 * D, 4 * C), 1) == want).astype(f32).astype(bf16)
        return dot(pick, v.tri_in[:, : 4 * C], ((1,), (1,))).astype(bf16)

    def operands(h, pair_norm):
        value = dot(chosen_weights(h, 0), pair_norm, ((1,), (1,)))
        value = value * jax.nn.sigmoid(dot(chosen_weights(h, 1), pair_norm, ((1,), (1,))))
        for n in range(D):
            for t in range(0, T, 2):
                two = [value[n * 2 * P4 : (n + 1) * 2 * P4, u * 128 : (u + 1) * 128] for u in (t, t + 1)]
                v.side_own[h, n // B, n // AX % BR, n % AX, t * 8 : t * 8 + 16, :] = jnp.concatenate(two, axis=0).astype(bf16)

    def share(own, everyone, send, recv, h):
        copies = []
        for n, (d, bo, a) in enumerate(peers):
            to = (p.res(d), p.br(bo), p.aux(a))
            copy = remote(
                own.at[(h, *to)], everyone.at[h, p.b, p.x, p.r] if everyone is v.side_all else everyone.at[h, p.r, p.b, p.x],
                send.at[h, n], recv.at[h, n], {"res": to[0], "br": to[1], "aux": to[2]},
            )
            copies.append(copy)
            sent.append(copy)
        return copies

    loads["couple"].wait()
    loads["tri_in"].wait()
    pair_norm = normalize(v.couple[...]).astype(bf16)
    v.pair_norm_s[...] = pair_norm
    operands(0, pair_norm)
    pl.semaphore_wait(barrier, D - 1)
    sides = {0: share(v.side_own, v.side_all, v.side_send, v.side_recv, 0)}

    for name in ("homolog", "symbols", "entries", "table"):
        loads[name].wait()
    here = v.entries[...].astype(f32)
    v.present[...] = jnp.zeros_like(v.present)
    v.present[0, :S, :] = jnp.concatenate([here] * (128 // A), axis=1)
    for g in range(A // N):
        pieces = [here[s : s + 1, g * N : (g + 1) * N] for s in range(S)]
        v.present[1, g : g + 1, :] = jnp.concatenate(pieces * (128 // (S * N)), axis=1)
    tokens = v.table.shape[0]
    for s in range(S):
        chosen = (iota((tokens, A), 0) == v.symbols[s : s + 1, :]).astype(f32)
        v.context_s[s * A : (s + 1) * A, :] = dot(jnp.transpose(chosen).astype(bf16), v.table[...], ((1,), (0,)))
    embedded = v.homolog[...].astype(f32) + v.context_s[...]
    v.embedded_s[...] = embedded
    normed_first = normalize(embedded).astype(bf16)
    v.rows_own[...] = normed_first
    for d in far_first(R):
        if d:
            for n, (src, dst) in enumerate(((v.rows_own, v.rows_all), (v.present.at[0], v.row_present))):
                copy = remote(src, dst.at[p.r], v.row_send.at[n, d], v.row_recv.at[n, d], {"res": p.res(d)})
                sent.append(copy)
                arriving["rows"].append(copy)
    loads["logit"].wait()
    v.bias_own[...] = dot(v.logit[...], pair_norm, ((1,), (1,)))
    for n, (bo, a) in enumerate(p.group()):
        to = {"br": p.br(bo), "aux": p.aux(a)}
        for m, (src, dst) in enumerate(((v.bias_own, v.bias_all), (v.present.at[1], v.col_present))):
            copy = remote(src, dst.at[p.b, p.x], v.grp_send.at[m, n], v.grp_recv.at[m, n], to)
            sent.append(copy)
            arriving["bias"].append(copy)
    for h in range(1, rounds):
        operands(h, v.pair_norm_s[...])
        sides[h] = share(v.side_own, v.side_all, v.side_send, v.side_recv, h)

    v.rows_all[p.r] = v.rows_own[...]
    v.row_present[p.r] = v.present[0]
    v.bias_all[p.b, p.x] = v.bias_own[...]
    v.col_present[p.b, p.x] = v.present[1]
    for h in range(rounds):
        v.side_all[h, p.b, p.x, p.r] = v.side_own[h, p.r, p.b, p.x]

    loads["row_in"].wait()
    query = dot(normed_first, v.row_in[:, :F], ((1,), (0,))).astype(bf16).astype(f32)
    row_gate = jax.nn.sigmoid(dot(normed_first, v.row_in[:, 3 * F :], ((1,), (0,))))
    v.gate_s[...] = jax.nn.sigmoid(dot(v.pair_norm_s[...], v.tri_in[:, 4 * C :], ((1,), (0,))))
    loads["amino"].wait()
    alive = v.amino[...].astype(f32)
    line = iota((128, 128), 0)
    lane = iota((128, 128), 1)
    alive_rows = jnp.sum(jnp.where(lane == line, alive, 0.0), axis=1, keepdims=True)
    depth = line % (R * T)
    alive_depth = jnp.sum(jnp.where(lane == depth // T * I + depth % T * Q + line // (R * T), alive, 0.0), axis=1, keepdims=True)
    v.depth_valid_s[...] = jnp.broadcast_to(alive_depth, (128, 128))
    v.valid_s[...] = alive_rows * alive

    for copy in arriving["bias"]:
        copy.wait_recv()
    for t in range(T):
        for q in range(Q):
            pieces = []
            for b in range(B):
                tile = v.bias_all[b // AX, b % AX, :, t * 128 : (t + 1) * 128]
                turn = (b - q) % Q * J
                pieces.append(pltpu.roll(tile, turn, 1) if turn else tile)
            row = (t * Q + q) * H
            v.bias_s[row : row + H, :] = joined(pieces, J)

    def triangle(h):
        for copy in sides[h]:
            copy.wait_recv()
        for z in range(R):
            for t in range(0, T, 2):
                rows = slice(t * 8, t * 8 + 16)
                pieces = [v.side_all[h, b // AX, b % AX, z, rows, :].astype(f32) for b in range(B)]
                for q, piece in enumerate(lane_exchange(pieces, J)):
                    v.side_s[q, z * T * 8 + t * 8 : z * T * 8 + t * 8 + 16, :] = piece
        for c in range(P4):
            left, right = [
                jnp.concatenate([v.side_s[q, pl.ds(side * P4 + c, R * T, stride=8), :] for q in range(Q)], axis=0)
                for side in range(2)
            ]
            left = (left * v.depth_valid_s[...]).astype(bf16)
            grid = dot(jnp.transpose(right).astype(bf16), left, ((1,), (0,))) * v.valid_s[...]
            for b in range(B):
                tiles = [grid[b * J + g * M : b * J + (g + 1) * M, :] for g in range(Q)]
                for n, tile in enumerate(lane_exchange(tiles, J)):
                    v.product_s[n, b // AX, b % AX, c * M : (c + 1) * M, :] = tile
        v.product_own[h] = v.product_s[...].astype(bf16)
        copies = share(v.product_own, v.product_all, v.product_send, v.product_recv, h)
        v.product_all[h, p.r, p.b, p.x] = v.product_own[h, p.r, p.b, p.x]
        return copies

    products = triangle(0)

    for copy in arriving["rows"]:
        copy.wait_recv()
    v.key_value_s[...] = (
        dot(v.rows_all[...].reshape(R * S * A, F), v.row_in[:, F : 3 * F], ((1,), (0,)))
        .astype(bf16)
        .reshape(R, S * A, 2 * F)
    )
    presence = joined([v.row_present[n] for n in range(R)], A)
    for s in range(S):
        mine = slice(s * A, (s + 1) * A)
        keys = v.key_value_s[:, mine, :F].reshape(R * A, F)
        values = v.key_value_s[:, mine, F:].reshape(R * A, F)
        scores = dot(by_head(query[mine], H).astype(bf16), keys, ((1,), (1,))) * scale
        scores = scores + v.bias_s[...] + masked_fill_value * (presence[s : s + 1] - 1.0)
        v.context_s[mine, :] = attend(scores, values, H)
    loads["row_exit"].wait()
    loads["col_in"].wait()
    row_mix = (row_gate * v.context_s[...]).astype(bf16)
    after_row = v.embedded_s[...] + dot(row_mix, v.row_exit[...], ((1,), (0,)))
    normed_second = normalize(after_row).astype(bf16)
    v.keys_own[...] = dot(normed_second, v.col_in[:, F : 3 * F], ((1,), (0,))).astype(bf16).reshape(S, A, 2 * F)

    def pass_on(a):
        origin = (p.b, p.aux_back(a))
        src = v.keys_own if a == 0 else v.keys_all.at[origin]
        for bo in range(1, BR):
            copy = remote(src, v.keys_all.at[origin], v.over_send.at[a, bo], v.over_recv.at[a, bo], {"br": p.br(bo)})
            sent.append(copy)
            arriving["keys"].append(copy)

    across = {}
    for a in range(1, AX):
        across[a] = remote(
            v.keys_own, v.keys_all.at[p.b, p.x], v.across_send.at[a], v.across_recv.at[a], {"aux": p.aux(a)}
        )
        sent.append(across[a])
    pass_on(0)
    v.keys_all[p.b, p.x] = v.keys_own[...]
    query = dot(normed_second, v.col_in[:, :F], ((1,), (0,))).astype(bf16).astype(f32)
    col_gate = jax.nn.sigmoid(dot(normed_second, v.col_in[:, 3 * F :], ((1,), (0,))))

    for h in range(1, rounds):
        products += triangle(h)
    for a in range(1, AX):
        across[a].wait_recv()
        pass_on(a)
    for copy in arriving["keys"]:
        copy.wait_recv()
    presence = joined([v.col_present[b // AX, b % AX] for b in range(B)], S * N)
    for g in range(A // N):
        keys = v.keys_all[:, :, :, g * N : (g + 1) * N, :F].reshape(B * S * N, F)
        values = v.keys_all[:, :, :, g * N : (g + 1) * N, F:].reshape(B * S * N, F)
        rows = jnp.concatenate([query[s * A + g * N : s * A + (g + 1) * N] for s in range(S)], axis=0)
        scores = dot(by_head(rows, H).astype(bf16), keys, ((1,), (1,))) * scale
        scores = scores + masked_fill_value * (presence[g : g + 1] - 1.0)
        scores = jnp.where(iota(scores.shape, 0) // H % N == iota(scores.shape, 1) % N, scores, -1e30)
        context = attend(scores, values, H)
        for s in range(S):
            v.context_s[s * A + g * N : s * A + (g + 1) * N, :] = context[s * N : (s + 1) * N]
    for name in ("col_exit", "feed_first", "feed_second", "tri_exit"):
        loads[name].wait()
    col_mix = (col_gate * v.context_s[...]).astype(bf16)
    after_col = after_row + dot(col_mix, v.col_exit[...], ((1,), (0,)))
    normed_third = normalize(after_col).astype(bf16)
    hidden = jnp.maximum(dot(normed_third, v.feed_first[...], ((1,), (0,))), 0.0).astype(bf16)
    v.alignment[...] = (after_col + dot(hidden, v.feed_second[...], ((1,), (0,)))).astype(bf16)

    for copy in products:
        copy.wait_recv()
    normed = normalize(v.product_all[...].astype(f32).reshape(C, M, 128), axis=0)
    v.final_s[...] = normed.reshape(C * M, 128)
    for m in range(M):
        turned = jnp.transpose(v.final_s[pl.ds(m, C, stride=M), :]).astype(bf16)
        update = dot(turned, v.tri_exit[...], ((1,), (0,)))
        for g in range(Q):
            v.update_s[pl.ds(g * M + m, I, stride=J), :] = update[g * I : (g + 1) * I]
    v.pair[...] = (v.couple[...].astype(f32) + v.gate_s[...] * v.update_s[...]).astype(bf16)
    for copy in sent:
        copy.wait_send()


def hand_over(alignment, pair, alignment_out, pair_out, sem):
    copies = [
        pltpu.make_async_copy(alignment, alignment_out, sem.at[0]),
        pltpu.make_async_copy(pair, pair_out, sem.at[1]),
    ]
    for copy in copies:
        copy.start()
    for copy in copies:
        copy.wait()


INPUTS = (
    "couple", "tri_in", "homolog", "symbols", "entries", "table", "logit", "amino", "row_in", "row_exit", "col_in",
    "col_exit", "feed_first", "feed_second", "tri_exit",
)


def far_first(count):
    return sorted(range(count), key=lambda d: -min(d, count - d))


def exchanged(sizes, inputs, dims):
    R, BR, AX = sizes
    B = BR * AX
    S, A, F, H, I, J, C, P4, T, N, rounds = dims
    M = J * J // 128
    peers = R * B - 1
    scratch = {name: pltpu.VMEM(inputs[name].shape, inputs[name].dtype) for name in INPUTS}
    for name, shape, kind in (
        ("side_own", (rounds, R, BR, AX, 8 * T, 128), bf16), ("side_all", (rounds, BR, AX, R, 8 * T, 128), bf16),
        ("side_s", (B, R * T * 8, 128), f32),
        ("product_s", (R, BR, AX, P4 * M, 128), f32), ("product_own", (rounds, R, BR, AX, P4 * M, 128), bf16),
        ("product_all", (rounds, R, BR, AX, P4 * M, 128), bf16),
        ("rows_own", (S * A, F), bf16), ("rows_all", (R, S * A, F), bf16),
        ("present", (2, 8, 128), f32), ("row_present", (R, 8, 128), f32), ("col_present", (BR, AX, 8, 128), f32),
        ("bias_own", (H, I * J), f32), ("bias_all", (BR, AX, H, I * J), f32), ("bias_s", (I * H, B * J), f32),
        ("keys_own", (S, A, 2 * F), bf16), ("keys_all", (BR, AX, S, A, 2 * F), bf16),
        ("key_value_s", (R, S * A, 2 * F), bf16), ("embedded_s", (S * A, F), f32), ("context_s", (S * A, F), f32),
        ("pair_norm_s", (I * J, C), bf16), ("gate_s", (I * J, C), f32),
        ("depth_valid_s", (128, 128), f32), ("valid_s", (128, 128), f32),
        ("final_s", (C * M, 128), f32), ("update_s", (I * J, C), f32),
    ):
        scratch[name] = pltpu.VMEM(shape, kind)
    for name, shape in (
        ("side_send", (rounds, peers)), ("side_recv", (rounds, peers)),
        ("product_send", (rounds, peers)), ("product_recv", (rounds, peers)),
        ("row_send", (2, R)), ("row_recv", (2, R)), ("grp_send", (2, B)), ("grp_recv", (2, B)),
        ("across_send", (AX,)), ("across_recv", (AX,)), ("over_send", (AX, BR)), ("over_recv", (AX, BR)),
        ("load_sem", (len(INPUTS),)),
    ):
        scratch[name] = pltpu.SemaphoreType.DMA(shape)
    names = [name + "_far" for name in INPUTS] + ["alignment", "pair", *scratch]
    vmem = pl.BlockSpec(memory_space=pltpu.VMEM)
    far = pl.BlockSpec(memory_space=pltpu.HBM)
    shapes = [jax.ShapeDtypeStruct((S * A, F), bf16), jax.ShapeDtypeStruct((I * J, C), bf16)]
    results = pl.pallas_call(
        functools.partial(exchange_kernel, sizes, dims, names),
        name="exchange",
        out_shape=shapes,
        in_specs=[far] * len(INPUTS),
        out_specs=[vmem] * 2,
        scratch_shapes=list(scratch.values()),
        compiler_params=pltpu.CompilerParams(
            collective_id=1, has_side_effects=True, vmem_limit_bytes=32 * 1024 * 1024
        ),
    )(*[pltpu.with_memory_space_constraint(inputs[name], pltpu.HBM) for name in INPUTS])
    return pl.pallas_call(
        hand_over,
        name="hand_over",
        out_shape=shapes,
        in_specs=[vmem] * 2,
        out_specs=[far] * 2,
        scratch_shapes=[pltpu.SemaphoreType.DMA((2,))],
        compiler_params=pltpu.CompilerParams(vmem_limit_bytes=4 * 1024 * 1024),
    )(*results)


def on_device(
    sizes,
    homolog_features,
    couple_features,
    symbol_ids,
    entry_present,
    amino_present,
    symbol_lookup_matrix,
    horizontal_entry_matrix,
    couple_logit_matrix,
    horizontal_exit_matrix,
    vertical_entry_matrix,
    vertical_exit_matrix,
    feedforward_first_matrix,
    feedforward_second_matrix,
    trimul_entry_matrix,
    trimul_exit_matrix,
):
    R, BR, AX = sizes
    B = BR * AX
    S, A, F = homolog_features.shape
    H = couple_logit_matrix.shape[1]
    I, J, C = couple_features.shape
    per = C // R
    T = I * J // 128
    N = 16
    P4 = 4
    if R == B == 128 // J and I == J and T % 2 == 0 and C % (P4 * R * B) == 0 and R * T * (128 // J) == 128:
        inputs = {
            "couple": couple_features.reshape(I * J, C), "tri_in": trimul_entry_matrix,
            "homolog": homolog_features.reshape(S * A, F), "symbols": symbol_ids, "entries": entry_present,
            "table": symbol_lookup_matrix, "logit": jnp.transpose(couple_logit_matrix),
            "amino": amino_present.reshape(1, -1), "row_in": horizontal_entry_matrix,
            "row_exit": horizontal_exit_matrix, "col_in": vertical_entry_matrix, "col_exit": vertical_exit_matrix,
            "feed_first": feedforward_first_matrix, "feed_second": feedforward_second_matrix,
            "tri_exit": trimul_exit_matrix,
        }
        alignment, pair = exchanged(sizes, inputs, (S, A, F, H, I, J, C, P4, T, N, C // (P4 * R * B)))
        return (alignment.reshape(S, A, F), pair.reshape(I, J, C))
    assert I == J and R == B and 128 % J == 0 and 128 % A == 0 and 128 % (S * N) == 0 and A % N == 0
    M = J // (128 // J)
    near = (
        homolog_features.reshape(S * A, F),
        couple_features.reshape(I * J, C),
        symbol_ids,
        entry_present,
        amino_present.reshape(1, -1),
        symbol_lookup_matrix,
        couple_logit_matrix,
        trimul_entry_matrix,
        trimul_exit_matrix,
    )
    far = (
        horizontal_entry_matrix,
        horizontal_exit_matrix,
        vertical_entry_matrix,
        vertical_exit_matrix,
        feedforward_first_matrix,
        feedforward_second_matrix,
    )
    vmem = pl.BlockSpec(memory_space=pltpu.VMEM)
    buffers = [
        ((S * A, F), bf16), ((H, I * J), f32), ((R, T, per, 128), bf16), ((R, T, per, 128), bf16),
        ((S, A, 2 * F), bf16), ((R, per * M, 128), bf16),
        ((R, S * A, F), bf16), ((R, 8, 128), f32), ((BR, AX, H, I * J), f32), ((BR, AX, 8, 128), f32),
        ((BR, AX, R, T, per, 128), bf16), ((R, T, per, 128), bf16), ((BR, AX, S, A, 2 * F), bf16),
        ((R, per * M, 128), bf16),
        *[(weight.shape, bf16) for weight in far], ((2, 8, 128), f32),
        ((S * A, F), f32), ((I * J, C), bf16), ((I * J, C), f32), ((I * H, B * J), f32),
        ((R, S * A, 2 * F), bf16), ((B, R * T * per, 128), f32), ((R * T * per, 128), f32),
        ((R, per * M, 128), f32), ((I * J, C), f32), ((S * A, F), f32),
    ]
    semaphores = [
        (5, R), (5, R), (2, B), (2, B), (R, AX), (R, AX), (R, AX, BR), (R, AX, BR),
        (AX,), (AX,), (AX, BR), (AX, BR), (len(far),),
    ]
    alignment, pair = pl.pallas_call(
        functools.partial(block_kernel, sizes, (S, A, F, H, I, J, C, per, T, N)),
        name="block",
        out_shape=[jax.ShapeDtypeStruct((S * A, F), bf16), jax.ShapeDtypeStruct((I * J, C), bf16)],
        in_specs=[vmem] * len(near) + [pl.BlockSpec(memory_space=pl.ANY)] * len(far),
        out_specs=[vmem] * 2,
        scratch_shapes=[pltpu.VMEM(*b) for b in buffers] + [pltpu.SemaphoreType.DMA(s) for s in semaphores],
        compiler_params=pltpu.CompilerParams(
            collective_id=1, has_side_effects=True, vmem_limit_bytes=60 * 1024 * 1024
        ),
    )(*near, *far)
    return (alignment.reshape(S, A, F), pair.reshape(I, J, C))


def solution(mesh):
    sizes = (mesh.shape["res"], mesh.shape["br"], mesh.shape["aux"])
    return jax.shard_map(
        functools.partial(on_device, sizes),
        mesh=mesh,
        in_specs=(
            P(("grp", "br", "aux"), "res", None),
            P(("grp", "res"), ("br", "aux"), None),
            P(("grp", "br", "aux"), "res"),
            P(("grp", "br", "aux"), "res"),
            P("grp"),
        )
        + (P(),) * 10,
        out_specs=(P(("grp", "br", "aux"), "res", None), P(("grp", "res"), ("br", "aux"), None)),
        check_vma=False,
    )
```

```python
import functools
import types

import jax
import jax.numpy as jnp
from jax import lax
from jax.experimental import pallas as pl
from jax.experimental.pallas import tpu as pltpu
from jax.sharding import PartitionSpec as P

epsilon = 1e-05
masked_fill_value = 1000000000.0
MESH = pl.DeviceIdType.MESH
f32 = jnp.float32
bf16 = jnp.bfloat16


def normalize(inputs, axis=-1):
    values = inputs.astype(f32)
    average = jnp.mean(values, axis=axis, keepdims=True)
    centred = values - average
    variance = jnp.mean(centred * centred, axis=axis, keepdims=True)
    return centred * lax.rsqrt(variance + epsilon)


def dot(a, b, contract):
    return lax.dot_general(a, b, (contract, ((), ())), preferred_element_type=f32)


class Peers:
    def __init__(self, sizes):
        self.R, self.BR, self.AX = sizes
        self.r = lax.axis_index("res")
        self.b = lax.axis_index("br")
        self.x = lax.axis_index("aux")

    def res(self, d):
        return lax.rem(self.r + d, self.R)

    def br(self, d):
        return lax.rem(self.b + d, self.BR)

    def aux(self, d):
        return lax.rem(self.x + d, self.AX)

    def res_back(self, d):
        return lax.rem(self.r + self.R - d, self.R)

    def aux_back(self, d):
        return lax.rem(self.x + self.AX - d, self.AX)

    def group(self):
        return [(bo, a) for bo in range(self.BR) for a in range(self.AX) if (bo, a) != (0, 0)]

    def greet(self):
        semaphore = pltpu.get_barrier_semaphore()
        for d in range(1, self.R):
            pl.semaphore_signal(semaphore, inc=1, device_id={"res": self.res(d)}, device_id_type=MESH)
        for bo, a in self.group():
            pl.semaphore_signal(
                semaphore, inc=1, device_id={"br": self.br(bo), "aux": self.aux(a)}, device_id_type=MESH
            )

    def met(self):
        pl.semaphore_wait(pltpu.get_barrier_semaphore(), self.R - 1 + self.BR * self.AX - 1)


def remote(src, dst, send, recv, device):
    copy = pltpu.make_async_remote_copy(
        src_ref=src, dst_ref=dst, send_sem=send, recv_sem=recv, device_id=device, device_id_type=MESH
    )
    copy.start()
    return copy


def iota(shape, axis):
    return lax.broadcasted_iota(jnp.int32, shape, axis)


def by_head(rows, heads):
    n, width = rows.shape
    mask = (iota((heads, width), 1) // (width // heads) == iota((heads, width), 0)).astype(f32)
    return (rows[:, None, :] * mask[None]).reshape(n * heads, width)


def from_head(rows, heads):
    n, width = rows.shape
    mask = (iota((heads, width), 1) // (width // heads) == iota((heads, width), 0)).astype(f32)
    return jnp.sum(rows.reshape(n // heads, heads, width) * mask[None], axis=1)


def attend(scores, values, heads):
    powers = jnp.exp(scores - jnp.max(scores, axis=-1, keepdims=True))
    total = jnp.sum(powers, axis=-1, keepdims=True)
    mixed = dot(powers.astype(bf16), values, ((1,), (0,)))
    return from_head(mixed / total, heads)


def joined(pieces, lanes):
    per_tile = 128 // lanes
    tiles = []
    for first in range(0, len(pieces), per_tile):
        tile = pieces[first]
        group = iota(tile.shape, 1) // lanes
        for k in range(1, min(per_tile, len(pieces) - first)):
            tile = jnp.where(group == k, pieces[first + k], tile)
        tiles.append(tile)
    return tiles[0] if len(tiles) == 1 else jnp.concatenate(tiles, axis=1)


def block_kernel(
    sizes, dims,
    homolog, couple, symbols, entries, amino, table, logit, tri_in, tri_exit,
    row_in_far, row_exit_far, col_in_far, col_exit_far, feed_first_far, feed_second_far,
    alignment, pair,
    rows_own, bias_own, left_own, right_own, keys_own, product_own,
    rows_all, row_present, bias_all, col_present, left_all, right_all, keys_all, product_all,
    row_in, row_exit, col_in, col_exit, feed_first, feed_second, present,
    embedded_s, pair_norm_s, gate_s, bias_s, key_value_s, left_s, right_s, product_s, update_s, context_s,
    res_send, res_recv, grp_send, grp_recv, aux_send, aux_recv, br_send, br_recv,
    across_send, across_recv, over_send, over_recv, weight_sem,
):
    p = Peers(sizes)
    R, BR, AX = sizes
    B = BR * AX
    S, A, F, H, I, J, C, per, T, N = dims
    scale = (F // H) ** (-0.5)
    Q = 128 // J
    M = J // Q
    p.greet()
    weights = []
    for n, (far, near) in enumerate(
        (
            (row_in_far, row_in),
            (row_exit_far, row_exit),
            (col_in_far, col_in),
            (col_exit_far, col_exit),
            (feed_first_far, feed_first),
            (feed_second_far, feed_second),
        )
    ):
        weights.append(pltpu.make_async_copy(far, near, weight_sem.at[n]))
        weights[n].start()
    sent = []
    arriving = {"rows": [], "bias": [], "right": [], "left": [], "keys": [], "product": []}

    pair_norm = normalize(couple[...]).astype(bf16)
    pair_norm_s[...] = pair_norm
    alive = jnp.broadcast_to(amino[...].astype(f32), (8, amino.shape[1])).astype(bf16)
    residue = iota((amino.shape[1], I * J), 0)
    flat = iota((amino.shape[1], I * J), 1)
    row_pick = (residue == p.r * I + flat // J).astype(f32).astype(bf16)
    col_pick = (residue == (p.b * AX + p.x) * J + flat % J).astype(f32).astype(bf16)
    pair_valid = (dot(alive, row_pick, ((1,), (0,))) * dot(alive, col_pick, ((1,), (0,))))[:1]
    turned_in = [jnp.transpose(tri_in[:, n * C : (n + 1) * C].astype(f32)).astype(bf16) for n in range(4)]
    for side, own in ((0, left_own), (1, right_own)):
        value = dot(turned_in[2 * side], pair_norm, ((1,), (1,)))
        sigma = jax.nn.sigmoid(dot(turned_in[2 * side + 1], pair_norm, ((1,), (1,))))
        value = sigma * value * pair_valid
        for n in range(R):
            for t in range(T):
                own[n, t] = value[n * per : (n + 1) * per, t * 128 : (t + 1) * 128].astype(bf16)
    bias_own[...] = dot(jnp.transpose(logit[...].astype(f32)).astype(bf16), pair_norm, ((1,), (1,)))
    here = entries[...].astype(f32)
    present[...] = jnp.zeros_like(present)
    present[0, :S, :] = jnp.concatenate([here] * (128 // A), axis=1)
    for g in range(A // N):
        pieces = [here[s : s + 1, g * N : (g + 1) * N] for s in range(S)]
        present[1, g : g + 1, :] = jnp.concatenate(pieces * (128 // (S * N)), axis=1)
    tokens = table.shape[0]
    for s in range(S):
        chosen = (iota((tokens, A), 0) == symbols[s : s + 1, :]).astype(f32)
        context_s[s * A : (s + 1) * A, :] = dot(jnp.transpose(chosen).astype(bf16), table[...], ((1,), (0,)))
    embedded = homolog[...].astype(f32) + context_s[...]
    embedded_s[...] = embedded
    normed_first = normalize(embedded).astype(bf16)
    rows_own[...] = normed_first

    p.met()

    def relay(d, a):
        origin = (p.b, p.aux_back(a), p.res_back(d))
        src = left_own.at[p.r] if (d, a) == (0, 0) else left_all.at[origin]
        for bo in range(1, BR):
            copy = remote(
                src, left_all.at[origin], br_send.at[d, a, bo], br_recv.at[d, a, bo], {"br": p.br(bo)}
            )
            sent.append(copy)
            arriving["left"].append(copy)

    def spread(d):
        origin = (p.b, p.x, p.res_back(d))
        src = left_own.at[p.r] if d == 0 else left_all.at[origin]
        copies = {}
        for a in range(1, AX):
            copies[a] = remote(
                src, left_all.at[origin], aux_send.at[d, a], aux_recv.at[d, a], {"aux": p.aux(a)}
            )
            sent.append(copies[a])
        relay(d, 0)
        return copies

    def to_res(index, kind, pairs):
        for d in range(1, R):
            for n, (src, dst) in enumerate(pairs(p.res(d))):
                copy = remote(
                    src, dst, res_send.at[index + n, d], res_recv.at[index + n, d], {"res": p.res(d)}
                )
                sent.append(copy)
                arriving[kind].append(copy)

    lefts = {}
    for d in range(1, R):
        lefts[d] = remote(
            left_own.at[p.res(d)], left_all.at[p.b, p.x, p.r], res_send.at[0, d], res_recv.at[0, d],
            {"res": p.res(d)},
        )
        sent.append(lefts[d])
    spreads = {0: spread(0)}
    to_res(1, "rows", lambda to: ((rows_own, rows_all.at[p.r]), (present.at[0], row_present.at[p.r])))
    for n, (bo, a) in enumerate(p.group()):
        to = {"br": p.br(bo), "aux": p.aux(a)}
        for m, (src, dst) in enumerate(((bias_own, bias_all), (present.at[1], col_present))):
            copy = remote(src, dst.at[p.b, p.x], grp_send.at[m, n], grp_recv.at[m, n], to)
            sent.append(copy)
            arriving["bias"].append(copy)
    to_res(3, "right", lambda to: ((right_own.at[to], right_all.at[p.r]),))
    rows_all[p.r] = rows_own[...]
    row_present[p.r] = present[0]
    bias_all[p.b, p.x] = bias_own[...]
    col_present[p.b, p.x] = present[1]
    left_all[p.b, p.x, p.r] = left_own[p.r]
    right_all[p.r] = right_own[p.r]

    weights[0].wait()
    query = dot(normed_first, row_in[:, :F], ((1,), (0,))).astype(bf16).astype(f32)
    row_gate = jax.nn.sigmoid(dot(normed_first, row_in[:, 3 * F :], ((1,), (0,))))
    gate_s[...] = jax.nn.sigmoid(dot(pair_norm, tri_in[:, 4 * C :], ((1,), (0,))))

    for d in range(1, R):
        lefts[d].wait_recv()
        spreads[d] = spread(d)
    for copy in arriving["bias"]:
        copy.wait_recv()
    for t in range(T):
        for q in range(Q):
            pieces = []
            for b in range(B):
                tile = bias_all[b // AX, b % AX, :, t * 128 : (t + 1) * 128]
                turn = (b - q) % Q * J
                pieces.append(pltpu.roll(tile, turn, 1) if turn else tile)
            row = (t * Q + q) * H
            bias_s[row : row + H, :] = joined(pieces, J)
    for d in range(R):
        for a in range(1, AX):
            spreads[d][a].wait_recv()
            relay(d, a)

    for copy in arriving["rows"]:
        copy.wait_recv()
    key_value_s[...] = (
        dot(rows_all[...].reshape(R * S * A, F), row_in[:, F : 3 * F], ((1,), (0,)))
        .astype(bf16)
        .reshape(R, S * A, 2 * F)
    )
    presence = joined([row_present[n] for n in range(R)], A)
    for s in range(S):
        mine = slice(s * A, (s + 1) * A)
        keys = key_value_s[:, mine, :F].reshape(R * A, F)
        values = key_value_s[:, mine, F:].reshape(R * A, F)
        scores = dot(by_head(query[mine], H).astype(bf16), keys, ((1,), (1,))) * scale
        scores = scores + bias_s[...] + masked_fill_value * (presence[s : s + 1] - 1.0)
        context_s[mine, :] = attend(scores, values, H)
    weights[1].wait()
    weights[2].wait()
    row_mix = (row_gate * context_s[...]).astype(bf16)
    after_row = embedded_s[...] + dot(row_mix, row_exit[...], ((1,), (0,)))
    normed_second = normalize(after_row).astype(bf16)
    keys_own[...] = dot(normed_second, col_in[:, F : 3 * F], ((1,), (0,))).astype(bf16).reshape(S, A, 2 * F)
    query = dot(normed_second, col_in[:, :F], ((1,), (0,))).astype(bf16).astype(f32)
    col_gate = jax.nn.sigmoid(dot(normed_second, col_in[:, 3 * F :], ((1,), (0,))))

    def pass_on(a):
        origin = (p.b, p.aux_back(a))
        src = keys_own if a == 0 else keys_all.at[origin]
        for bo in range(1, BR):
            copy = remote(src, keys_all.at[origin], over_send.at[a, bo], over_recv.at[a, bo], {"br": p.br(bo)})
            sent.append(copy)
            arriving["keys"].append(copy)

    across = {}
    for a in range(1, AX):
        across[a] = remote(
            keys_own, keys_all.at[p.b, p.x], across_send.at[a], across_recv.at[a], {"aux": p.aux(a)}
        )
        sent.append(across[a])
    pass_on(0)
    keys_all[p.b, p.x] = keys_own[...]

    for copy in arriving["right"]:
        copy.wait_recv()
    right_s[...] = right_all[...].astype(f32).reshape(R * T * per, 128)
    for copy in arriving["left"]:
        copy.wait_recv()
    for b in range(B):
        left_s[b] = left_all[b // AX, b % AX].astype(f32).reshape(R * T * per, 128)
    wide = iota((J, 128), 1) // J
    lane = iota((M, 128), 1)

    def channel(c, carry):
        pick = pl.ds(c, R * T, stride=per)
        right = jnp.transpose(right_s[pick, :]).astype(bf16)
        lefts = jnp.concatenate([left_s[b, pick, :].astype(bf16) for b in range(B)], axis=1)
        grid = dot(right, lefts, ((1,), (0,)))
        for b in range(B):
            tile = grid[:, b * 128 : (b + 1) * 128]
            folded = tile[:J]
            for q in range(1, Q):
                folded = jnp.where(wide == q, tile[q * J : (q + 1) * J], folded)
            pieces = [folded[g * M : (g + 1) * M] for g in range(Q)]
            turn = J
            while turn < 128:
                low = (lane & turn) == 0
                pieces = [
                    jnp.where(low, pieces[k], pieces[k + 1])
                    + pltpu.roll(jnp.where(low, pieces[k + 1], pieces[k]), turn, 1)
                    for k in range(0, len(pieces), 2)
                ]
                turn *= 2
            product_s[b, pl.ds(pl.multiple_of(c * M, M), M), :] = pieces[0]
        return carry

    lax.fori_loop(0, per, channel, 0, unroll=4)
    product_own[...] = product_s[...].astype(bf16)
    for a in range(1, AX):
        across[a].wait_recv()
        pass_on(a)
    to_res(4, "product", lambda to: ((product_own.at[to], product_all.at[p.r]),))
    product_all[p.r] = product_own[p.r]

    for copy in arriving["keys"]:
        copy.wait_recv()
    presence = joined([col_present[b // AX, b % AX] for b in range(B)], S * N)
    for g in range(A // N):
        keys = keys_all[:, :, :, g * N : (g + 1) * N, :F].reshape(B * S * N, F)
        values = keys_all[:, :, :, g * N : (g + 1) * N, F:].reshape(B * S * N, F)
        rows = jnp.concatenate([query[s * A + g * N : s * A + (g + 1) * N] for s in range(S)], axis=0)
        scores = dot(by_head(rows, H).astype(bf16), keys, ((1,), (1,))) * scale
        scores = scores + masked_fill_value * (presence[g : g + 1] - 1.0)
        scores = jnp.where(iota(scores.shape, 0) // H % N == iota(scores.shape, 1) % N, scores, -1e30)
        context = attend(scores, values, H)
        for s in range(S):
            context_s[s * A + g * N : s * A + (g + 1) * N, :] = context[s * N : (s + 1) * N]
    for n in (3, 4, 5):
        weights[n].wait()
    col_mix = (col_gate * context_s[...]).astype(bf16)
    after_col = after_row + dot(col_mix, col_exit[...], ((1,), (0,)))
    normed_third = normalize(after_col).astype(bf16)
    hidden = jnp.maximum(dot(normed_third, feed_first[...], ((1,), (0,))), 0.0).astype(bf16)
    alignment[...] = (after_col + dot(hidden, feed_second[...], ((1,), (0,)))).astype(bf16)

    for copy in arriving["product"]:
        copy.wait_recv()
    normed = normalize(product_all[...].astype(f32).reshape(C, M, 128), axis=0)
    final_s = left_s.at[0]
    final_s[: C * M, :] = normed.reshape(C * M, 128)
    for m in range(M):
        turned = jnp.transpose(final_s[pl.ds(m, C, stride=M), :]).astype(bf16)
        update = dot(turned, tri_exit[...], ((1,), (0,)))
        for g in range(Q):
            update_s[pl.ds(g * M + m, I, stride=J), :] = update[g * I : (g + 1) * I]
    pair[...] = (couple[...].astype(f32) + gate_s[...] * update_s[...]).astype(bf16)
    for copy in sent:
        copy.wait_send()


def lane_exchange(pieces, width):
    count = len(pieces)
    step = 1
    while step < count:
        lower = (iota(pieces[0].shape, pieces[0].ndim - 1) // width // step) % 2 == 0
        axis = pieces[0].ndim - 1
        turned = list(pieces)
        for n in range(count):
            if n // step % 2 == 0:
                first, second = pieces[n], pieces[n + step]
                turned[n] = jnp.where(lower, first, pltpu.roll(second, step * width, axis))
                turned[n + step] = jnp.where(lower, pltpu.roll(first, 128 - step * width, axis), second)
        pieces = turned
        step *= 2
    return pieces


def exchange_kernel(sizes, dims, names, *refs):
    v = types.SimpleNamespace(**dict(zip(names, refs, strict=True)))
    p = Peers(sizes)
    R, BR, AX = sizes
    B = BR * AX
    D = R * B
    S, A, F, H, I, J, C, P4, T, N, rounds = dims
    scale = (F // H) ** (-0.5)
    Q = 128 // J
    M = J // Q
    peers = [(d, bo, a) for d in far_first(R) for bo in range(BR) for a in range(AX) if (d, bo, a) != (0, 0, 0)]
    loads = {}
    for n, name in enumerate(INPUTS):
        loads[name] = pltpu.make_async_copy(getattr(v, name + "_far"), getattr(v, name), v.load_sem.at[n])
        loads[name].start()
    barrier = pltpu.get_barrier_semaphore()
    for d, bo, a in peers:
        pl.semaphore_signal(
            barrier, inc=1, device_id={"res": p.res(d), "br": p.br(bo), "aux": p.aux(a)}, device_id_type=MESH
        )
    sent = []
    arriving = {"rows": [], "bias": [], "keys": []}

    def chosen_weights(h, gate):
        row = iota((2 * P4 * D, 1), 0)
        want = (2 * (row // P4 % 2) + gate) * C + h * P4 * D + row // (2 * P4) * P4 + row % P4
        pick = (iota((2 * P4 * D, 4 * C), 1) == want).astype(f32).astype(bf16)
        return dot(pick, v.tri_in[:, : 4 * C], ((1,), (1,))).astype(bf16)

    def operands(h, pair_norm):
        value = dot(chosen_weights(h, 0), pair_norm, ((1,), (1,)))
        value = value * jax.nn.sigmoid(dot(chosen_weights(h, 1), pair_norm, ((1,), (1,))))
        for n in range(D):
            for t in range(0, T, 2):
                two = [value[n * 2 * P4 : (n + 1) * 2 * P4, u * 128 : (u + 1) * 128] for u in (t, t + 1)]
                v.side_own[h, n // B, n // AX % BR, n % AX, t * 8 : t * 8 + 16, :] = jnp.concatenate(two, axis=0).astype(bf16)

    def share(own, everyone, send, recv, h, wanted=lambda a: True):
        copies = []
        for n, (d, bo, a) in enumerate(peers):
            if not wanted(a):
                continue
            to = (p.res(d), p.br(bo), p.aux(a))
            copy = remote(
                own.at[(h, *to)], everyone.at[h, p.b, p.x, p.r] if everyone is v.side_all else everyone.at[h, p.r, p.b, p.x],
                send.at[h, n], recv.at[h, n], {"res": to[0], "br": to[1], "aux": to[2]},
            )
            copies.append(copy)
            sent.append(copy)
        return copies

    def embed():
        for name in ("homolog", "symbols", "entries", "table"):
            loads[name].wait()
        here = v.entries[...].astype(f32)
        v.present[...] = jnp.zeros_like(v.present)
        v.present[0, :S, :] = jnp.concatenate([here] * (128 // A), axis=1)
        for g in range(A // N):
            pieces = [here[s : s + 1, g * N : (g + 1) * N] for s in range(S)]
            v.present[1, g : g + 1, :] = jnp.concatenate(pieces * (128 // (S * N)), axis=1)
        tokens = v.table.shape[0]
        for s in range(S):
            chosen = (iota((tokens, A), 0) == v.symbols[s : s + 1, :]).astype(f32)
            v.context_s[s * A : (s + 1) * A, :] = dot(jnp.transpose(chosen).astype(bf16), v.table[...], ((1,), (0,)))
        embedded = v.homolog[...].astype(f32) + v.context_s[...]
        v.embedded_s[...] = embedded
        v.rows_own[...] = normalize(embedded).astype(bf16)

    half = R // 2
    upper = p.r // half
    base = upper * half
    gateway = p.r == half - 1 + upper
    foreign = [(1 - upper) * half + k for k in range(half)]
    mates = [base + lax.rem(p.r - base + e, half) for e in range(1, half)]

    def row_copy(origin, to, send, own):
        pairs = ((v.rows_own, v.rows_all), (v.present.at[0], v.row_present))
        return [
            pltpu.make_async_remote_copy(
                src_ref=src if own else dst.at[origin], dst_ref=dst.at[origin],
                send_sem=send.at[n], recv_sem=v.row_recv.at[n, origin], device_id={"res": to}, device_id_type=MESH,
            )
            for n, (src, dst) in enumerate(pairs)
        ]

    forwards = [
        row_copy(origin, to, v.forward_send.at[k, e], False)
        for k, origin in enumerate(foreign)
        for e, to in enumerate(mates)
    ]

    def received(origins):
        for origin in origins:
            for copy in row_copy(origin, p.r, v.row_send.at[0], False):
                copy.wait_recv()

    loads["couple"].wait()
    loads["tri_in"].wait()
    pair_norm = normalize(v.couple[...]).astype(bf16)
    v.pair_norm_s[...] = pair_norm
    embed()
    operands(0, pair_norm)
    pl.semaphore_wait(barrier, D - 1)
    for n, to in enumerate([half - upper, *mates]):
        for copy in row_copy(p.r, to, v.row_send.at[n], True):
            copy.start()
            sent.append(copy)
    loads["logit"].wait()
    v.bias_own[...] = dot(v.logit[...], pair_norm, ((1,), (1,)))
    for n, (bo, a) in enumerate(p.group()):
        to = {"br": p.br(bo), "aux": p.aux(a)}
        for m, (src, dst) in enumerate(((v.bias_own, v.bias_all), (v.present.at[1], v.col_present))):
            copy = remote(src, dst.at[p.b, p.x], v.grp_send.at[m, n], v.grp_recv.at[m, n], to)
            sent.append(copy)
            arriving["bias"].append(copy)
    sides = {0: share(v.side_own, v.side_all, v.side_send, v.side_recv, 0)}
    for h in range(1, rounds):
        operands(h, v.pair_norm_s[...])

    v.rows_all[p.r] = v.rows_own[...]
    v.row_present[p.r] = v.present[0]
    v.bias_all[p.b, p.x] = v.bias_own[...]
    v.col_present[p.b, p.x] = v.present[1]
    for h in range(rounds):
        v.side_all[h, p.b, p.x, p.r] = v.side_own[h, p.r, p.b, p.x]

    loads["row_in"].wait()
    normed_first = v.rows_own[...]
    query = dot(normed_first, v.row_in[:, :F], ((1,), (0,))).astype(bf16).astype(f32)
    row_gate = jax.nn.sigmoid(dot(normed_first, v.row_in[:, 3 * F :], ((1,), (0,))))
    v.gate_s[...] = jax.nn.sigmoid(dot(v.pair_norm_s[...], v.tri_in[:, 4 * C :], ((1,), (0,))))
    loads["amino"].wait()
    alive = v.amino[...].astype(f32)
    line = iota((128, 128), 0)
    lane = iota((128, 128), 1)
    alive_rows = jnp.sum(jnp.where(lane == line, alive, 0.0), axis=1, keepdims=True)
    depth = line % (R * T)
    alive_depth = jnp.sum(jnp.where(lane == depth // T * I + depth % T * Q + line // (R * T), alive, 0.0), axis=1, keepdims=True)
    v.depth_valid_s[...] = jnp.broadcast_to(alive_depth, (128, 128))
    v.valid_s[...] = alive_rows * alive

    @pl.when(gateway)
    def _():
        received(foreign)
        for copies in forwards:
            for copy in copies:
                copy.start()

    for h in range(1, rounds):
        sides[h] = share(v.side_own, v.side_all, v.side_send, v.side_recv, h)
    for copy in arriving["bias"]:
        copy.wait_recv()
    for t in range(T):
        for q in range(Q):
            pieces = []
            for b in range(B):
                tile = v.bias_all[b // AX, b % AX, :, t * 128 : (t + 1) * 128]
                turn = (b - q) % Q * J
                pieces.append(pltpu.roll(tile, turn, 1) if turn else tile)
            row = (t * Q + q) * H
            v.bias_s[row : row + H, :] = joined(pieces, J)

    def triangle(h):
        for copy in sides[h]:
            copy.wait_recv()
        for z in range(R):
            for t in range(0, T, 2):
                rows = slice(t * 8, t * 8 + 16)
                pieces = [v.side_all[h, b // AX, b % AX, z, rows, :].astype(f32) for b in range(B)]
                for q, piece in enumerate(lane_exchange(pieces, J)):
                    v.side_s[q, z * T * 8 + t * 8 : z * T * 8 + t * 8 + 16, :] = piece
        for c in range(P4):
            left, right = [
                jnp.concatenate([v.side_s[q, pl.ds(side * P4 + c, R * T, stride=8), :] for q in range(Q)], axis=0)
                for side in range(2)
            ]
            left = (left * v.depth_valid_s[...]).astype(bf16)
            grid = dot(jnp.transpose(right).astype(bf16), left, ((1,), (0,))) * v.valid_s[...]
            for b in range(B):
                tiles = [grid[b * J + g * M : b * J + (g + 1) * M, :] for g in range(Q)]
                for n, tile in enumerate(lane_exchange(tiles, J)):
                    v.product_s[n, b // AX, b % AX, c * M : (c + 1) * M, :] = tile
        v.product_own[h] = v.product_s[...].astype(bf16)
        copies = share(v.product_own, v.product_all, v.product_send, v.product_recv, h)
        v.product_all[h, p.r, p.b, p.x] = v.product_own[h, p.r, p.b, p.x]
        return copies

    @pl.when(jnp.logical_not(gateway))
    def _():
        received(foreign)

    received(mates)
    v.key_value_s[...] = (
        dot(v.rows_all[...].reshape(R * S * A, F), v.row_in[:, F : 3 * F], ((1,), (0,)))
        .astype(bf16)
        .reshape(R, S * A, 2 * F)
    )
    presence = joined([v.row_present[n] for n in range(R)], A)
    for s in range(S):
        mine = slice(s * A, (s + 1) * A)
        keys = v.key_value_s[:, mine, :F].reshape(R * A, F)
        values = v.key_value_s[:, mine, F:].reshape(R * A, F)
        scores = dot(by_head(query[mine], H).astype(bf16), keys, ((1,), (1,))) * scale
        scores = scores + v.bias_s[...] + masked_fill_value * (presence[s : s + 1] - 1.0)
        v.context_s[mine, :] = attend(scores, values, H)
    loads["row_exit"].wait()
    loads["col_in"].wait()
    row_mix = (row_gate * v.context_s[...]).astype(bf16)
    after_row = v.embedded_s[...] + dot(row_mix, v.row_exit[...], ((1,), (0,)))
    normed_second = normalize(after_row).astype(bf16)
    v.keys_own[...] = dot(normed_second, v.col_in[:, F : 3 * F], ((1,), (0,))).astype(bf16).reshape(S, A, 2 * F)

    def pass_on(a):
        origin = (p.b, p.aux_back(a))
        src = v.keys_own if a == 0 else v.keys_all.at[origin]
        for bo in range(1, BR):
            copy = remote(src, v.keys_all.at[origin], v.over_send.at[a, bo], v.over_recv.at[a, bo], {"br": p.br(bo)})
            sent.append(copy)
            arriving["keys"].append(copy)

    across = {}
    for a in range(1, AX):
        across[a] = remote(
            v.keys_own, v.keys_all.at[p.b, p.x], v.across_send.at[a], v.across_recv.at[a], {"aux": p.aux(a)}
        )
        sent.append(across[a])
    pass_on(0)
    v.keys_all[p.b, p.x] = v.keys_own[...]
    query = dot(normed_second, v.col_in[:, :F], ((1,), (0,))).astype(bf16).astype(f32)
    col_gate = jax.nn.sigmoid(dot(normed_second, v.col_in[:, 3 * F :], ((1,), (0,))))

    products = triangle(0)
    for a in range(1, AX):
        across[a].wait_recv()
        pass_on(a)
    for h in range(1, rounds):
        products += triangle(h)
    for copy in arriving["keys"]:
        copy.wait_recv()
    presence = joined([v.col_present[b // AX, b % AX] for b in range(B)], S * N)
    for g in range(A // N):
        keys = v.keys_all[:, :, :, g * N : (g + 1) * N, :F].reshape(B * S * N, F)
        values = v.keys_all[:, :, :, g * N : (g + 1) * N, F:].reshape(B * S * N, F)
        rows = jnp.concatenate([query[s * A + g * N : s * A + (g + 1) * N] for s in range(S)], axis=0)
        scores = dot(by_head(rows, H).astype(bf16), keys, ((1,), (1,))) * scale
        scores = scores + masked_fill_value * (presence[g : g + 1] - 1.0)
        scores = jnp.where(iota(scores.shape, 0) // H % N == iota(scores.shape, 1) % N, scores, -1e30)
        context = attend(scores, values, H)
        for s in range(S):
            v.context_s[s * A + g * N : s * A + (g + 1) * N, :] = context[s * N : (s + 1) * N]
    for name in ("col_exit", "feed_first", "feed_second", "tri_exit"):
        loads[name].wait()
    col_mix = (col_gate * v.context_s[...]).astype(bf16)
    after_col = after_row + dot(col_mix, v.col_exit[...], ((1,), (0,)))
    normed_third = normalize(after_col).astype(bf16)
    hidden = jnp.maximum(dot(normed_third, v.feed_first[...], ((1,), (0,))), 0.0).astype(bf16)
    v.alignment[...] = (after_col + dot(hidden, v.feed_second[...], ((1,), (0,)))).astype(bf16)

    waiting = len(sent) - (rounds - 1) * (D - 1)
    for copy in sent[:waiting]:
        copy.wait_send()

    @pl.when(gateway)
    def _():
        for copies in forwards:
            for copy in copies:
                copy.wait_send()

    for copy in products:
        copy.wait_recv()
    normed = normalize(v.product_all[...].astype(f32).reshape(C, M, 128), axis=0)
    v.final_s[...] = normed.reshape(C * M, 128)
    for m in range(M):
        turned = jnp.transpose(v.final_s[pl.ds(m, C, stride=M), :]).astype(bf16)
        update = dot(turned, v.tri_exit[...], ((1,), (0,)))
        for g in range(Q):
            v.update_s[pl.ds(g * M + m, I, stride=J), :] = update[g * I : (g + 1) * I]
    v.pair[...] = (v.couple[...].astype(f32) + v.gate_s[...] * v.update_s[...]).astype(bf16)
    for copy in sent[waiting:]:
        copy.wait_send()


def hand_over(alignment, pair, alignment_out, pair_out, sem):
    copies = [
        pltpu.make_async_copy(alignment, alignment_out, sem.at[0]),
        pltpu.make_async_copy(pair, pair_out, sem.at[1]),
    ]
    for copy in copies:
        copy.start()
    for copy in copies:
        copy.wait()


INPUTS = (
    "couple", "tri_in", "homolog", "symbols", "entries", "table", "logit", "amino", "row_in", "row_exit", "col_in",
    "col_exit", "feed_first", "feed_second", "tri_exit",
)


def far_first(count):
    return sorted(range(count), key=lambda d: -min(d, count - d))


def exchanged(sizes, inputs, dims):
    R, BR, AX = sizes
    B = BR * AX
    S, A, F, H, I, J, C, P4, T, N, rounds = dims
    M = J * J // 128
    peers = R * B - 1
    scratch = {name: pltpu.VMEM(inputs[name].shape, inputs[name].dtype) for name in INPUTS}
    for name, shape, kind in (
        ("side_own", (rounds, R, BR, AX, 8 * T, 128), bf16), ("side_all", (rounds, BR, AX, R, 8 * T, 128), bf16),
        ("side_s", (B, R * T * 8, 128), f32),
        ("product_s", (R, BR, AX, P4 * M, 128), f32), ("product_own", (rounds, R, BR, AX, P4 * M, 128), bf16),
        ("product_all", (rounds, R, BR, AX, P4 * M, 128), bf16),
        ("rows_own", (S * A, F), bf16), ("rows_all", (R, S * A, F), bf16),
        ("present", (2, 8, 128), f32), ("row_present", (R, 8, 128), f32), ("col_present", (BR, AX, 8, 128), f32),
        ("bias_own", (H, I * J), f32), ("bias_all", (BR, AX, H, I * J), f32), ("bias_s", (I * H, B * J), f32),
        ("keys_own", (S, A, 2 * F), bf16), ("keys_all", (BR, AX, S, A, 2 * F), bf16),
        ("key_value_s", (R, S * A, 2 * F), bf16), ("embedded_s", (S * A, F), f32), ("context_s", (S * A, F), f32),
        ("pair_norm_s", (I * J, C), bf16), ("gate_s", (I * J, C), f32),
        ("depth_valid_s", (128, 128), f32), ("valid_s", (128, 128), f32),
        ("final_s", (C * M, 128), f32), ("update_s", (I * J, C), f32),
    ):
        scratch[name] = pltpu.VMEM(shape, kind)
    for name, shape in (
        ("side_send", (rounds, peers)), ("side_recv", (rounds, peers)),
        ("product_send", (rounds, peers)), ("product_recv", (rounds, peers)),
        ("row_send", (R // 2, 2)), ("row_recv", (2, R)), ("forward_send", (R // 2, R // 2, 2)), ("grp_send", (2, B)), ("grp_recv", (2, B)),
        ("across_send", (AX,)), ("across_recv", (AX,)), ("over_send", (AX, BR)), ("over_recv", (AX, BR)),
        ("load_sem", (len(INPUTS),)),
    ):
        scratch[name] = pltpu.SemaphoreType.DMA(shape)
    names = [name + "_far" for name in INPUTS] + ["alignment", "pair", *scratch]
    vmem = pl.BlockSpec(memory_space=pltpu.VMEM)
    far = pl.BlockSpec(memory_space=pltpu.HBM)
    shapes = [jax.ShapeDtypeStruct((S * A, F), bf16), jax.ShapeDtypeStruct((I * J, C), bf16)]
    results = pl.pallas_call(
        functools.partial(exchange_kernel, sizes, dims, names),
        name="exchange",
        out_shape=shapes,
        in_specs=[far] * len(INPUTS),
        out_specs=[vmem] * 2,
        scratch_shapes=list(scratch.values()),
        compiler_params=pltpu.CompilerParams(
            collective_id=1, has_side_effects=True, vmem_limit_bytes=32 * 1024 * 1024
        ),
    )(*[pltpu.with_memory_space_constraint(inputs[name], pltpu.HBM) for name in INPUTS])
    return pl.pallas_call(
        hand_over,
        name="hand_over",
        out_shape=shapes,
        in_specs=[vmem] * 2,
        out_specs=[far] * 2,
        scratch_shapes=[pltpu.SemaphoreType.DMA((2,))],
        compiler_params=pltpu.CompilerParams(vmem_limit_bytes=4 * 1024 * 1024),
    )(*results)


def on_device(
    sizes,
    homolog_features,
    couple_features,
    symbol_ids,
    entry_present,
    amino_present,
    symbol_lookup_matrix,
    horizontal_entry_matrix,
    couple_logit_matrix,
    horizontal_exit_matrix,
    vertical_entry_matrix,
    vertical_exit_matrix,
    feedforward_first_matrix,
    feedforward_second_matrix,
    trimul_entry_matrix,
    trimul_exit_matrix,
):
    R, BR, AX = sizes
    B = BR * AX
    S, A, F = homolog_features.shape
    H = couple_logit_matrix.shape[1]
    I, J, C = couple_features.shape
    per = C // R
    T = I * J // 128
    N = 16
    P4 = 4
    if R == B == 128 // J and I == J and T % 2 == 0 and C % (P4 * R * B) == 0 and R * T * (128 // J) == 128:
        inputs = {
            "couple": couple_features.reshape(I * J, C), "tri_in": trimul_entry_matrix,
            "homolog": homolog_features.reshape(S * A, F), "symbols": symbol_ids, "entries": entry_present,
            "table": symbol_lookup_matrix, "logit": jnp.transpose(couple_logit_matrix),
            "amino": amino_present.reshape(1, -1), "row_in": horizontal_entry_matrix,
            "row_exit": horizontal_exit_matrix, "col_in": vertical_entry_matrix, "col_exit": vertical_exit_matrix,
            "feed_first": feedforward_first_matrix, "feed_second": feedforward_second_matrix,
            "tri_exit": trimul_exit_matrix,
        }
        alignment, pair = exchanged(sizes, inputs, (S, A, F, H, I, J, C, P4, T, N, C // (P4 * R * B)))
        return (alignment.reshape(S, A, F), pair.reshape(I, J, C))
    assert I == J and R == B and 128 % J == 0 and 128 % A == 0 and 128 % (S * N) == 0 and A % N == 0
    M = J // (128 // J)
    near = (
        homolog_features.reshape(S * A, F),
        couple_features.reshape(I * J, C),
        symbol_ids,
        entry_present,
        amino_present.reshape(1, -1),
        symbol_lookup_matrix,
        couple_logit_matrix,
        trimul_entry_matrix,
        trimul_exit_matrix,
    )
    far = (
        horizontal_entry_matrix,
        horizontal_exit_matrix,
        vertical_entry_matrix,
        vertical_exit_matrix,
        feedforward_first_matrix,
        feedforward_second_matrix,
    )
    vmem = pl.BlockSpec(memory_space=pltpu.VMEM)
    buffers = [
        ((S * A, F), bf16), ((H, I * J), f32), ((R, T, per, 128), bf16), ((R, T, per, 128), bf16),
        ((S, A, 2 * F), bf16), ((R, per * M, 128), bf16),
        ((R, S * A, F), bf16), ((R, 8, 128), f32), ((BR, AX, H, I * J), f32), ((BR, AX, 8, 128), f32),
        ((BR, AX, R, T, per, 128), bf16), ((R, T, per, 128), bf16), ((BR, AX, S, A, 2 * F), bf16),
        ((R, per * M, 128), bf16),
        *[(weight.shape, bf16) for weight in far], ((2, 8, 128), f32),
        ((S * A, F), f32), ((I * J, C), bf16), ((I * J, C), f32), ((I * H, B * J), f32),
        ((R, S * A, 2 * F), bf16), ((B, R * T * per, 128), f32), ((R * T * per, 128), f32),
        ((R, per * M, 128), f32), ((I * J, C), f32), ((S * A, F), f32),
    ]
    semaphores = [
        (5, R), (5, R), (2, B), (2, B), (R, AX), (R, AX), (R, AX, BR), (R, AX, BR),
        (AX,), (AX,), (AX, BR), (AX, BR), (len(far),),
    ]
    alignment, pair = pl.pallas_call(
        functools.partial(block_kernel, sizes, (S, A, F, H, I, J, C, per, T, N)),
        name="block",
        out_shape=[jax.ShapeDtypeStruct((S * A, F), bf16), jax.ShapeDtypeStruct((I * J, C), bf16)],
        in_specs=[vmem] * len(near) + [pl.BlockSpec(memory_space=pl.ANY)] * len(far),
        out_specs=[vmem] * 2,
        scratch_shapes=[pltpu.VMEM(*b) for b in buffers] + [pltpu.SemaphoreType.DMA(s) for s in semaphores],
        compiler_params=pltpu.CompilerParams(
            collective_id=1, has_side_effects=True, vmem_limit_bytes=60 * 1024 * 1024
        ),
    )(*near, *far)
    return (alignment.reshape(S, A, F), pair.reshape(I, J, C))


def solution(mesh):
    sizes = (mesh.shape["res"], mesh.shape["br"], mesh.shape["aux"])
    return jax.shard_map(
        functools.partial(on_device, sizes),
        mesh=mesh,
        in_specs=(
            P(("grp", "br", "aux"), "res", None),
            P(("grp", "res"), ("br", "aux"), None),
            P(("grp", "br", "aux"), "res"),
            P(("grp", "br", "aux"), "res"),
            P("grp"),
        )
        + (P(),) * 10,
        out_specs=(P(("grp", "br", "aux"), "res", None), P(("grp", "res"), ("br", "aux"), None)),
        check_vma=False,
    )
```
